128 devices in a mesh: ep: 32 (over z, x, core), tp: 4 (over y).
Axes of the slice: x: 4, y: 4, z: 4, core: 2. Of those that a mesh axis runs over, the one named last changes fastest.
Arguments:
- weights: bfloat16 [32, 2048, 7168], P('ep', None, 'tp'), may hold values from -6 to 6
- probes: bfloat16 [32, 7168, 256], P('ep', 'tp'), may hold values from -0.0625 to 0.0625
- pairing: int32 [32], replicated, may hold values from 0 to 31, each once
Outputs:
- basis: float32 [32, 2048, 256], P('ep', 'tp')
- factors: bfloat16 [32, 256, 7168], P('ep', None, 'tp')
The draws below stay inside these ranges and needn't reach their ends.
Inputs may be any that keep to these rules, and one draw needn't show every extreme that they name: `pairing`: entries 2i and 2i+1 name the two experts of pair i; every expert appears exactly once.
All inputs are finite; a program needn't handle non-finite values.
Results may differ from the reference program's by a relative error of at most 0.022.
Values may be sent and summed in bfloat16 or wider, within the bound.
No kernel may reach another device: no remote copies, remote signals or barrier semaphores. Data moves between devices by JAX's collectives and lax.ppermute only.
A program may use at most 64 MiB of HBM per device.

```python
import math
import jax
import jax.numpy as jnp
from jax import lax

D = 7168
FF = 2048
R = 256
POWER = 2
EXPERTS = 32


def draw_weights(key, part):
    value_key = jax.random.fold_in(jax.random.fold_in(key, 11), 0)
    values = jax.random.normal(value_key, (EXPERTS, FF, D), jnp.float32)
    return jnp.clip(values, -6.0, 6.0).astype(jnp.bfloat16)


def level_of(stream_key, extent, cuts, least, top_value):
    gain = 1.0
    for axis_at, parts in cuts:
        draws = jax.random.uniform(jax.random.fold_in(jax.random.fold_in(stream_key, 6), axis_at), (parts,), jnp.float32, least / len(cuts), top_value / len(cuts))
        gain = gain * jnp.repeat(jnp.exp(draws), extent[axis_at] // parts).reshape((-1,) + (1,) * (len(extent) - 1 - axis_at))
    return gain


def gaussian(own_key, dims, deviation, bound, shards=(), kind=jnp.bfloat16):
    factor_of = level_of(own_key, dims, shards, -0.22, 0.18) if shards else 1.0
    values = jax.random.normal(own_key, dims, jnp.float32) * deviation * factor_of
    return jnp.minimum(jnp.maximum(values, -bound), bound).astype(kind)


def setup_inputs(seed: int = 0) -> dict:
    key_list = jax.random.split(jax.random.key(seed), 4)
    weights = draw_weights(jax.random.fold_in(key_list[3], 71), 0)
    probes = gaussian(key_list[1], (EXPERTS, D, R), D ** -0.5, 0.0625, ((0, 32), (1, 4)))
    pairing = jax.random.permutation(key_list[2], EXPERTS).astype(jnp.int32)
    return {"weights": weights, "probes": probes, "pairing": pairing}


def pair_mixer(pairing):
    expert_count = pairing.shape[0]
    expert_ids = jnp.arange(expert_count, dtype=jnp.int32)
    leaders = (pairing[0::2][:, None] == expert_ids[None, :]).astype(jnp.float32)
    followers = (pairing[1::2][:, None] == expert_ids[None, :]).astype(jnp.float32)
    cross = jnp.dot(leaders.T, followers, precision=lax.Precision.HIGHEST)
    return jnp.eye(expert_count, dtype=jnp.float32) + cross + cross.T

def sketch_one(operands):
    weight, probe = operands
    return jnp.dot(weight.astype(jnp.float32), probe.astype(jnp.float32), preferred_element_type=jnp.float32)

def power_one(operands):
    weight, sketch = operands
    back_proj = jnp.dot(weight.T.astype(jnp.float32), sketch.astype(jnp.float32), preferred_element_type=jnp.float32).astype(jnp.bfloat16)
    return jnp.dot(weight.astype(jnp.float32), back_proj.astype(jnp.float32), preferred_element_type=jnp.float32) / D

def factor_one(operands):
    columns, weight = operands
    return jnp.dot(columns.T.astype(jnp.float32), weight.astype(jnp.float32), preferred_element_type=jnp.float32).astype(jnp.bfloat16)

def solve_one(lower, sketch):
    return jax.scipy.linalg.solve_triangular(lower, sketch.T, lower=True).T

def reference(weights, probes, pairing):
    pair_weights = pair_mixer(pairing)
    partial_value = lax.map(sketch_one, (weights, probes))
    paired_sketch = None
    for sweep in range(POWER + 1):
        if sweep > 0:
            partial_value = lax.map(power_one, (weights, paired_sketch))
        paired_sketch = jnp.einsum('ef,fnr->enr', pair_weights, partial_value, precision=lax.Precision.HIGHEST).astype(jnp.bfloat16)
    sketch_wide = paired_sketch.astype(jnp.float32)
    gram = jnp.einsum('enr,ens->ers', sketch_wide, sketch_wide, precision=lax.Precision.HIGHEST)
    lower = jnp.linalg.cholesky(gram)
    basis_cols = jax.vmap(solve_one)(lower, sketch_wide)
    basis = basis_cols * math.sqrt(FF)
    factors = lax.map(factor_one, (basis_cols.astype(jnp.bfloat16), weights))
    return (basis, factors)
```

```python
import math

import jax
import jax.numpy as jnp
from jax import lax
from jax.experimental import pallas as pl
from jax.experimental.pallas import tpu as pltpu
from jax.sharding import PartitionSpec as P

D = 7168
FF = 2048
POWER = 2
F32 = jnp.float32
BF16 = jnp.bfloat16
HIGHEST = lax.Precision.HIGHEST
BLOCK = 64
TILE = 256
VMEM_LIMIT = 40 * 1024 * 1024


def params():
    return pltpu.CompilerParams(vmem_limit_bytes=VMEM_LIMIT)


def vmem_spec():
    return pl.BlockSpec(memory_space=pltpu.VMEM)


def any_spec():
    return pl.BlockSpec(memory_space=pl.ANY)


def smem_spec():
    return pl.BlockSpec(memory_space=pltpu.SMEM)


def mm(a, b):
    return jnp.dot(a, b, preferred_element_type=F32)


def row_copies(weights, held, sems):
    rows = held.shape[0]
    return [
        pltpu.make_async_copy(
            weights.at[pl.ds(s, TILE), :], held.at[pl.ds(s, TILE), :], sems.at[n]
        )
        for n, s in enumerate(range(0, rows, TILE))
    ]


def column_copies(weights, held, sems):
    columns = held.shape[1]
    return [
        pltpu.make_async_copy(
            weights.at[:, pl.ds(s, TILE)], held.at[:, pl.ds(s, TILE)], sems.at[n]
        )
        for n, s in enumerate(range(0, columns, TILE))
    ]


def first_kernel(weights, probes, out, held, sems):
    copies = row_copies(weights, held, sems)
    for copy in copies:
        copy.start()
    for n, copy in enumerate(copies):
        copy.wait()
        s = n * TILE
        out[s : s + TILE, :] = mm(held[s : s + TILE, :], probes[...]).astype(BF16)


def power_kernel(weights, sketch, out, held, turned, back, sems):
    copies = column_copies(weights, held, sems)
    for copy in copies:
        copy.start()
    turned[...] = sketch[...].T
    for n, copy in enumerate(copies):
        copy.wait()
        s = n * TILE
        back[s : s + TILE, :] = mm(turned[...], held[:, s : s + TILE]).astype(BF16).T
    for s in range(0, out.shape[0], TILE):
        out[s : s + TILE, :] = (mm(held[s : s + TILE, :], back[...]) * (1.0 / D)).astype(BF16)


def pair_kernel(pairing, received, out):
    tp_count = out.shape[0] // pairing.shape[0]

    def total(expert):
        rows = received[pl.ds(expert * tp_count, tp_count)].astype(F32)
        return jnp.sum(rows, axis=0)

    for i in range(pairing.shape[0] // 2):
        a = pairing[2 * i]
        b = pairing[2 * i + 1]
        both = (total(a) + total(b)).astype(BF16)
        spread = jnp.broadcast_to(both[None], (tp_count,) + both.shape)
        out[pl.ds(a * tp_count, tp_count)] = spread
        out[pl.ds(b * tp_count, tp_count)] = spread


def factor_block(work):
    sublane = lax.broadcasted_iota(jnp.int32, (8, 2 * BLOCK), 0)

    def row(x, i):
        return jnp.broadcast_to(x[i : i + 1, :], x.shape)

    def column(x, c):
        return jnp.broadcast_to(x[:, c : c + 1], x.shape)

    count = BLOCK // 8
    groups = [work[8 * g : 8 * g + 8, :] for g in range(count)]
    for p in range(count):
        columns = {
            g: [column(groups[g], 8 * p + i) for i in range(8)] for g in range(p, count)
        }
        pivots = jnp.ones_like(groups[p])
        for i in range(8):
            pivot = row(columns[p][i], i)
            pivots = jnp.where(sublane == i, pivot, pivots)
            inverse = 1.0 / pivot
            across = [row(columns[p][c], i) for c in range(i + 1, 8)]
            pivot_row = row(groups[p], i)
            for g in range(p, count):
                if g == p and i == 7:
                    continue
                scaled = columns[g][i] * inverse
                if g == p:
                    scaled = jnp.where(sublane > i, scaled, 0.0)
                for n, c in enumerate(range(i + 1, 8)):
                    columns[g][c] = columns[g][c] - scaled * across[n]
                groups[g] = groups[g] - scaled * pivot_row
        work[8 * p : 8 * p + 8, :] = groups[p] * lax.rsqrt(pivots)


def inverse_factor(gram, inverse, work):
    size = gram.shape[0]

    def identity(n):
        rows = lax.broadcasted_iota(jnp.int32, (n, n), 0)
        columns = lax.broadcasted_iota(jnp.int32, (n, n), 1)
        return jnp.where(rows == columns, 1.0, 0.0).astype(F32)

    inverse[...] = identity(size)
    for s in range(0, size, BLOCK):
        e = s + BLOCK
        work[:, 0:BLOCK] = gram[s:e, s:e]
        work[:, BLOCK : 2 * BLOCK] = identity(BLOCK)
        factor_block(work)
        block = work[:, BLOCK : 2 * BLOCK]
        done = jnp.dot(block, inverse[s:e, :], precision=HIGHEST, preferred_element_type=F32)
        inverse[s:e, :] = done
        if e < size:
            upper = jnp.dot(block, gram[s:e, :], precision=HIGHEST, preferred_element_type=F32)
            left = upper[:, e:]
            turned = (((0,), (0,)), ((), ()))
            gram[e:, :] = gram[e:, :] - lax.dot_general(
                left, upper, turned, precision=HIGHEST, preferred_element_type=F32
            )
            inverse[e:, :] = inverse[e:, :] - lax.dot_general(
                left, done, turned, precision=HIGHEST, preferred_element_type=F32
            )


def final_kernel(
    start, weights, sketch, basis, factors, held, turned, mixed, gram, inverse, work, sems
):
    copies = column_copies(weights, held, sems)
    for copy in copies:
        copy.start()
    turned[...] = sketch[...].T
    gram[...] = mm(turned[...], sketch[...])
    inverse_factor(gram, inverse, work)
    high = inverse[...].astype(BF16)
    low = (inverse[...] - high.astype(F32)).astype(BF16)
    for s in range(0, sketch.shape[0], TILE):
        part = turned[:, s : s + TILE]
        mixed[:, s : s + TILE] = (mm(high, part) + mm(low, part)).astype(BF16)
    own_count = basis.shape[0]
    own = sketch[pl.ds(pl.multiple_of(start[0] * own_count, own_count), own_count), :]
    basis[...] = (mm(own, high.T) + mm(own, low.T)) * math.sqrt(FF)
    for n, copy in enumerate(copies):
        copy.wait()
        s = n * TILE
        factors[:, s : s + TILE] = mm(mixed[...], held[:, s : s + TILE]).astype(BF16)


def exchange(value):
    return lax.all_to_all(value, ("ep", "tp"), split_axis=0, concat_axis=0, tiled=True)


def per_device(weights, probes, pairing):
    weight_block = weights[0]
    probe_block = probes[0]
    rows, columns = weight_block.shape
    rank = probe_block.shape[1]
    device_count = lax.axis_size("ep") * lax.axis_size("tp")
    own_count = rows // lax.axis_size("tp")
    held = pltpu.VMEM((rows, columns), BF16)
    row_sems = pltpu.SemaphoreType.DMA((rows // TILE,))
    column_sems = pltpu.SemaphoreType.DMA((columns // TILE,))
    sketch_shape = jax.ShapeDtypeStruct((rows, rank), BF16)
    chunks = (device_count, rows // device_count, rank)

    def relay(partial_value):
        received = exchange(partial_value.reshape(chunks))
        paired = pl.pallas_call(
            pair_kernel,
            out_shape=jax.ShapeDtypeStruct(chunks, BF16),
            in_specs=[smem_spec(), vmem_spec()],
            out_specs=vmem_spec(),
            name="pair",
        )(pairing, received)
        return exchange(paired).reshape(rows, rank)

    partial_value = pl.pallas_call(
        first_kernel,
        out_shape=sketch_shape,
        in_specs=[any_spec(), vmem_spec()],
        out_specs=vmem_spec(),
        scratch_shapes=[held, row_sems],
        compiler_params=params(),
        name="first",
    )(weight_block, probe_block)
    sketch = relay(partial_value)
    for _ in range(POWER):
        partial_value = pl.pallas_call(
            power_kernel,
            out_shape=sketch_shape,
            in_specs=[any_spec(), vmem_spec()],
            out_specs=vmem_spec(),
            scratch_shapes=[
                held,
                pltpu.VMEM((rank, rows), BF16),
                pltpu.VMEM((columns, rank), BF16),
                column_sems,
            ],
            compiler_params=params(),
            name="power",
        )(weight_block, sketch)
        sketch = relay(partial_value)
    start = lax.axis_index("tp").reshape(1).astype(jnp.int32)
    basis, factors = pl.pallas_call(
        final_kernel,
        out_shape=(
            jax.ShapeDtypeStruct((own_count, rank), F32),
            jax.ShapeDtypeStruct((rank, columns), BF16),
        ),
        in_specs=[smem_spec(), any_spec(), vmem_spec()],
        out_specs=(vmem_spec(), vmem_spec()),
        scratch_shapes=[
            held,
            pltpu.VMEM((rank, rows), BF16),
            pltpu.VMEM((rank, rows), BF16),
            pltpu.VMEM((rank, rank), F32),
            pltpu.VMEM((rank, rank), F32),
            pltpu.VMEM((BLOCK, 2 * BLOCK), F32),
            column_sems,
        ],
        compiler_params=params(),
        name="final",
    )(start, weight_block, sketch)
    return (basis[None], factors[None])


def solution(mesh):
    placed = (P("ep", None, "tp"), P("ep", "tp", None), P())
    return jax.shard_map(
        per_device,
        mesh=mesh,
        in_specs=placed,
        out_specs=(P("ep", "tp", None), P("ep", None, "tp")),
        check_vma=False,
    )
```

```python
import math

import jax
import jax.numpy as jnp
from jax import lax
from jax.experimental import pallas as pl
from jax.experimental.pallas import tpu as pltpu
from jax.sharding import PartitionSpec as P

D = 7168
FF = 2048
POWER = 2
F32 = jnp.float32
BF16 = jnp.bfloat16
HIGHEST = lax.Precision.HIGHEST
BLOCK = 64
TILE = 256
VMEM_LIMIT = 24 * 1024 * 1024


def params():
    return pltpu.CompilerParams(vmem_limit_bytes=VMEM_LIMIT)


def vmem_spec():
    return pl.BlockSpec(memory_space=pltpu.VMEM)


def smem_spec():
    return pl.BlockSpec(memory_space=pltpu.SMEM)


def mm(a, b):
    return jnp.dot(a, b, preferred_element_type=F32)


def first_kernel(weights, probes, out):
    for s in range(0, out.shape[0], 2 * TILE):
        out[s : s + 2 * TILE, :] = mm(weights[s : s + 2 * TILE, :], probes[...]).astype(BF16)


def power_kernel(weights, sketch, out, turned, back):
    turned[...] = sketch[...].T
    for s in range(0, weights.shape[1], TILE):
        back[s : s + TILE, :] = mm(turned[...], weights[:, s : s + TILE]).astype(BF16).T
    for s in range(0, out.shape[0], 2 * TILE):
        rows = weights[s : s + 2 * TILE, :]
        out[s : s + 2 * TILE, :] = (mm(rows, back[...]) * (1.0 / D)).astype(BF16)


def pair_kernel(pairing, received, out):
    tp_count = out.shape[0] // pairing.shape[0]

    def total(expert):
        rows = received[pl.ds(expert * tp_count, tp_count)].astype(F32)
        return jnp.sum(rows, axis=0)

    for i in range(pairing.shape[0] // 2):
        a = pairing[2 * i]
        b = pairing[2 * i + 1]
        both = (total(a) + total(b)).astype(BF16)
        spread = jnp.broadcast_to(both[None], (tp_count,) + both.shape)
        out[pl.ds(a * tp_count, tp_count)] = spread
        out[pl.ds(b * tp_count, tp_count)] = spread


def factor_block(work):
    sublane = lax.broadcasted_iota(jnp.int32, (8, 2 * BLOCK), 0)

    def row(x, i):
        return jnp.broadcast_to(x[i : i + 1, :], x.shape)

    def column(x, c):
        return jnp.broadcast_to(x[:, c : c + 1], x.shape)

    count = BLOCK // 8
    groups = [work[8 * g : 8 * g + 8, :] for g in range(count)]
    for p in range(count):
        columns = {
            g: [column(groups[g], 8 * p + i) for i in range(8)] for g in range(p, count)
        }
        pivots = jnp.ones_like(groups[p])
        for i in range(8):
            pivot = row(columns[p][i], i)
            pivots = jnp.where(sublane == i, pivot, pivots)
            inverse = 1.0 / pivot
            across = [row(columns[p][c], i) for c in range(i + 1, 8)]
            pivot_row = row(groups[p], i)
            for g in range(p, count):
                if g == p and i == 7:
                    continue
                scaled = columns[g][i] * inverse
                if g == p:
                    scaled = jnp.where(sublane > i, scaled, 0.0)
                for n, c in enumerate(range(i + 1, 8)):
                    columns[g][c] = columns[g][c] - scaled * across[n]
                groups[g] = groups[g] - scaled * pivot_row
        work[8 * p : 8 * p + 8, :] = groups[p] * lax.rsqrt(pivots)


def inverse_factor(gram, inverse, work):
    size = gram.shape[0]

    def identity(n):
        rows = lax.broadcasted_iota(jnp.int32, (n, n), 0)
        columns = lax.broadcasted_iota(jnp.int32, (n, n), 1)
        return jnp.where(rows == columns, 1.0, 0.0).astype(F32)

    inverse[...] = identity(size)
    for s in range(0, size, BLOCK):
        e = s + BLOCK
        work[:, 0:BLOCK] = gram[s:e, s:e]
        work[:, BLOCK : 2 * BLOCK] = identity(BLOCK)
        factor_block(work)
        block = work[:, BLOCK : 2 * BLOCK]
        done = jnp.dot(block, inverse[s:e, :], precision=HIGHEST, preferred_element_type=F32)
        inverse[s:e, :] = done
        if e < size:
            upper = jnp.dot(block, gram[s:e, :], precision=HIGHEST, preferred_element_type=F32)
            left = upper[:, e:]
            turned = (((0,), (0,)), ((), ()))
            gram[e:, :] = gram[e:, :] - lax.dot_general(
                left, upper, turned, precision=HIGHEST, preferred_element_type=F32
            )
            inverse[e:, :] = inverse[e:, :] - lax.dot_general(
                left, done, turned, precision=HIGHEST, preferred_element_type=F32
            )


def final_kernel(
    start, weights, sketch, basis, factors, turned, mixed, gram, inverse, work
):
    turned[...] = sketch[...].T
    gram[...] = mm(turned[...], sketch[...])
    inverse_factor(gram, inverse, work)
    high = inverse[...].astype(BF16)
    low = (inverse[...] - high.astype(F32)).astype(BF16)
    for s in range(0, sketch.shape[0], TILE):
        part = turned[:, s : s + TILE]
        mixed[:, s : s + TILE] = (mm(high, part) + mm(low, part)).astype(BF16)
    own_count = basis.shape[0]
    own = sketch[pl.ds(pl.multiple_of(start[0] * own_count, own_count), own_count), :]
    basis[...] = (mm(own, high.T) + mm(own, low.T)) * math.sqrt(FF)
    for s in range(0, weights.shape[1], TILE):
        factors[:, s : s + TILE] = mm(mixed[...], weights[:, s : s + TILE]).astype(BF16)


def exchange(value):
    return lax.all_to_all(value, ("ep", "tp"), split_axis=0, concat_axis=0, tiled=True)


def per_device(weights, probes, pairing):
    weight_block = weights[0]
    probe_block = probes[0]
    rows, columns = weight_block.shape
    rank = probe_block.shape[1]
    device_count = lax.axis_size("ep") * lax.axis_size("tp")
    own_count = rows // lax.axis_size("tp")
    sketch_shape = jax.ShapeDtypeStruct((rows, rank), BF16)
    chunks = (device_count, rows // device_count, rank)

    def relay(partial_value):
        received = exchange(partial_value.reshape(chunks))
        paired = pl.pallas_call(
            pair_kernel,
            out_shape=jax.ShapeDtypeStruct(chunks, BF16),
            in_specs=[smem_spec(), vmem_spec()],
            out_specs=vmem_spec(),
            compiler_params=params(),
            name="pair",
        )(pairing, received)
        return exchange(paired).reshape(rows, rank)

    partial_value = pl.pallas_call(
        first_kernel,
        out_shape=sketch_shape,
        in_specs=[vmem_spec(), vmem_spec()],
        out_specs=vmem_spec(),
        compiler_params=params(),
        name="first",
    )(weight_block, probe_block)
    start = lax.axis_index("tp").reshape(1).astype(jnp.int32)
    partial_value, start = lax.optimization_barrier((partial_value, start))
    sketch = relay(partial_value)
    for _ in range(POWER):
        partial_value = pl.pallas_call(
            power_kernel,
            out_shape=sketch_shape,
            in_specs=[vmem_spec(), vmem_spec()],
            out_specs=vmem_spec(),
            scratch_shapes=[
                pltpu.VMEM((rank, rows), BF16),
                pltpu.VMEM((columns, rank), BF16),
            ],
            compiler_params=params(),
            name="power",
        )(weight_block, sketch)
        sketch = relay(partial_value)
    basis, factors = pl.pallas_call(
        final_kernel,
        out_shape=(
            jax.ShapeDtypeStruct((own_count, rank), F32),
            jax.ShapeDtypeStruct((rank, columns), BF16),
        ),
        in_specs=[smem_spec(), vmem_spec(), vmem_spec()],
        out_specs=(vmem_spec(), vmem_spec()),
        scratch_shapes=[
            pltpu.VMEM((rank, rows), BF16),
            pltpu.VMEM((rank, rows), BF16),
            pltpu.VMEM((rank, rank), F32),
            pltpu.VMEM((rank, rank), F32),
            pltpu.VMEM((BLOCK, 2 * BLOCK), F32),
        ],
        compiler_params=params(),
        name="final",
    )(start, weight_block, sketch)
    return (basis[None], factors[None])


def solution(mesh):
    placed = (P("ep", None, "tp"), P("ep", "tp", None), P())
    return jax.shard_map(
        per_device,
        mesh=mesh,
        in_specs=placed,
        out_specs=(P("ep", "tp", None), P("ep", None, "tp")),
        check_vma=False,
    )
```

```python
import math

import jax
import jax.numpy as jnp
from jax import lax
from jax.experimental import pallas as pl
from jax.experimental.pallas import tpu as pltpu
from jax.sharding import PartitionSpec as P

D = 7168
FF = 2048
POWER = 2
F32 = jnp.float32
BF16 = jnp.bfloat16
HIGHEST = lax.Precision.HIGHEST
BLOCK = 128
TILE = 256
VMEM_LIMIT = 24 * 1024 * 1024


def params():
    return pltpu.CompilerParams(vmem_limit_bytes=VMEM_LIMIT)


def vmem_spec():
    return pl.BlockSpec(memory_space=pltpu.VMEM)


def any_spec():
    return pl.BlockSpec(memory_space=pl.ANY)


def smem_spec():
    return pl.BlockSpec(memory_space=pltpu.SMEM)


def mm(a, b):
    return jnp.dot(a, b, preferred_element_type=F32)


def first_kernel(weights, probes, out):
    for s in range(0, out.shape[0], 2 * TILE):
        out[s : s + 2 * TILE, :] = mm(weights[s : s + 2 * TILE, :], probes[...]).astype(BF16)


def power_kernel(weights, sketch, out, turned, back):
    turned[...] = sketch[...].T
    for s in range(0, weights.shape[1], TILE):
        back[s : s + TILE, :] = mm(turned[...], weights[:, s : s + TILE]).astype(BF16).T
    for s in range(0, out.shape[0], 2 * TILE):
        rows = weights[s : s + 2 * TILE, :]
        out[s : s + 2 * TILE, :] = (mm(rows, back[...]) * (1.0 / D)).astype(BF16)


def pair_kernel(pairing, received, out):
    tp_count = out.shape[0] // pairing.shape[0]

    def total(expert):
        rows = received[pl.ds(expert * tp_count, tp_count)].astype(F32)
        return jnp.sum(rows, axis=0)

    for i in range(pairing.shape[0] // 2):
        a = pairing[2 * i]
        b = pairing[2 * i + 1]
        both = (total(a) + total(b)).astype(BF16)
        spread = jnp.broadcast_to(both[None], (tp_count,) + both.shape)
        out[pl.ds(a * tp_count, tp_count)] = spread
        out[pl.ds(b * tp_count, tp_count)] = spread


def exact(a, b):
    return jnp.dot(a, b, precision=HIGHEST, preferred_element_type=F32)


def exact_turned(a, b):
    turned = (((0,), (0,)), ((), ()))
    return lax.dot_general(a, b, turned, precision=HIGHEST, preferred_element_type=F32)


def identity(n):
    rows = lax.broadcasted_iota(jnp.int32, (n, n), 0)
    columns = lax.broadcasted_iota(jnp.int32, (n, n), 1)
    return jnp.where(rows == columns, 1.0, 0.0).astype(F32)


def factor_block(work, beside):
    lanes = work.shape[0]
    halves = range(work.shape[1] // lanes)
    count = lanes // 8
    sublane = lax.broadcasted_iota(jnp.int32, (8, lanes), 0)
    ones = jnp.ones((8, lanes), F32)

    def row(x, i):
        return jnp.broadcast_to(x[i : i + 1, :], x.shape)

    def column(x, c):
        return jnp.broadcast_to(x[:, c : c + 1], x.shape)

    def place(g, h):
        return slice(8 * g, 8 * g + 8), slice(lanes * h, lanes * h + lanes)

    groups = [[work[place(g, h)] for h in halves] for g in range(count)]
    for p in range(0, count, 2):
        if beside:
            beside.pop(0)()
        base = 8 * p
        reduced = [list(groups[p]), list(groups[p + 1])]
        final = [list(groups[p]), list(groups[p + 1])]
        columns = [[column(groups[p + q][0], base + i) for q in range(2)] for i in range(16)]
        inverses = [ones, ones]
        pivots = [ones, ones]
        for i in range(16):
            q, r = divmod(i, 8)
            pivot = row(columns[i][q], r)
            inverse = 1.0 / pivot
            pivots[q] = jnp.where(sublane == r, pivot, pivots[q])
            inverses[q] = jnp.where(sublane == r, inverse, inverses[q])
            scaled = [columns[i][0] * inverse, columns[i][1] * inverse]
            scaled[q] = jnp.where(sublane == r, 0.0, scaled[q])
            for c in range(i + 1, 16):
                across = row(columns[c][q], r)
                columns[c] = [columns[c][k] - scaled[k] * across for k in range(2)]
            for h in halves:
                pivot_row = row(reduced[q][h], r)
                final[q][h] = jnp.where(sublane == r, pivot_row, final[q][h])
                for k in range(2):
                    reduced[k][h] = reduced[k][h] - scaled[k] * pivot_row
        for q in range(2):
            scale = lax.rsqrt(pivots[q])
            for h in halves:
                work[place(p + q, h)] = final[q][h] * scale
                reduced[q][h] = reduced[q][h] * inverses[q]
        solved = [[row(reduced[c // 8][h], c % 8) for h in halves] for c in range(16)]
        for g in range(p + 2, count):
            left = [column(groups[g][0], base + c) for c in range(16)]
            for h in halves:
                terms = [left[c] * solved[c][h] for c in range(16)]
                while len(terms) > 1:
                    terms = [terms[k] + terms[k + 1] for k in range(0, len(terms), 2)]
                groups[g][h] = groups[g][h] - terms[0]
    while beside:
        beside.pop(0)()


def inverse_factor(gram, inverse, work, beside):
    n = BLOCK
    upper_left, lower_left = slice(0, n), slice(n, 2 * n)
    work[:, :n] = gram[upper_left, :n]
    work[:, n:] = identity(n)
    share = (len(beside) + 1) // 2
    factor_block(work, beside[:share])
    top = work[:, n:]
    cross = exact(top, gram[upper_left, n:])
    work[:, :n] = gram[lower_left, n:] - exact_turned(cross, cross)
    work[:, n:] = identity(n)

    def fill():
        inverse[upper_left, :n] = top
        inverse[upper_left, n:] = jnp.zeros((n, n), F32)
        inverse[lower_left, :n] = exact_turned(cross, top)

    factor_block(work, [fill] + beside[share:])
    bottom = work[:, n:]
    inverse[lower_left, :n] = -exact(bottom, inverse[lower_left, :n])
    inverse[lower_left, n:] = bottom


def final_kernel(
    start,
    weights,
    sketch,
    basis,
    factors,
    turned,
    high_part,
    low_part,
    gram,
    inverse,
    work,
    own_basis,
    own_factors,
    sems,
):
    columns = weights.shape[1]
    turned[...] = sketch[...].T
    gram[...] = mm(turned[...], sketch[...])

    def project(s):
        def run():
            product = mm(turned[...], weights[:, s : s + TILE])
            high = product.astype(BF16)
            high_part[:, s : s + TILE] = high
            low_part[:, s : s + TILE] = (product - high.astype(F32)).astype(BF16)

        return run

    inverse_factor(gram, inverse, work, [project(s) for s in range(0, columns, TILE)])
    high = inverse[...].astype(BF16)
    low = (inverse[...] - high.astype(F32)).astype(BF16)
    copies = []
    for n, s in enumerate(range(0, columns, TILE)):
        part = high_part[:, s : s + TILE]
        rest = mm(low, part) + mm(high, low_part[:, s : s + TILE])
        own_factors[:, s : s + TILE] = (mm(high, part) + rest).astype(BF16)
        place = pl.ds(s, TILE)
        copies.append(
            pltpu.make_async_copy(own_factors.at[:, place], factors.at[:, place], sems.at[n])
        )
        copies[-1].start()
    own_count = own_basis.shape[0]
    own = sketch[pl.ds(pl.multiple_of(start[0] * own_count, own_count), own_count), :]
    own_basis[...] = (mm(own, high.T) + mm(own, low.T)) * math.sqrt(FF)
    copies.append(pltpu.make_async_copy(own_basis, basis, sems.at[len(copies)]))
    copies[-1].start()
    for copy in copies:
        copy.wait()


def exchange(value):
    return lax.all_to_all(value, ("ep", "tp"), split_axis=0, concat_axis=0, tiled=True)


def per_device(weights, probes, pairing):
    weight_block = weights[0]
    probe_block = probes[0]
    rows, columns = weight_block.shape
    rank = probe_block.shape[1]
    device_count = lax.axis_size("ep") * lax.axis_size("tp")
    own_count = rows // lax.axis_size("tp")
    sketch_shape = jax.ShapeDtypeStruct((rows, rank), BF16)
    chunks = (device_count, rows // device_count, rank)

    def relay(partial_value):
        received = exchange(partial_value.reshape(chunks))
        paired = pl.pallas_call(
            pair_kernel,
            out_shape=jax.ShapeDtypeStruct(chunks, BF16),
            in_specs=[smem_spec(), vmem_spec()],
            out_specs=vmem_spec(),
            compiler_params=params(),
            name="pair",
        )(pairing, received)
        return exchange(paired).reshape(rows, rank)

    partial_value = pl.pallas_call(
        first_kernel,
        out_shape=sketch_shape,
        in_specs=[vmem_spec(), vmem_spec()],
        out_specs=vmem_spec(),
        compiler_params=params(),
        name="first",
    )(weight_block, probe_block)
    start = lax.axis_index("tp").reshape(1).astype(jnp.int32)
    partial_value, start = lax.optimization_barrier((partial_value, start))
    sketch = relay(partial_value)
    for _ in range(POWER):
        partial_value = pl.pallas_call(
            power_kernel,
            out_shape=sketch_shape,
            in_specs=[vmem_spec(), vmem_spec()],
            out_specs=vmem_spec(),
            scratch_shapes=[
                pltpu.VMEM((rank, rows), BF16),
                pltpu.VMEM((columns, rank), BF16),
            ],
            compiler_params=params(),
            name="power",
        )(weight_block, sketch)
        sketch = relay(partial_value)
    basis, factors = pl.pallas_call(
        final_kernel,
        out_shape=(
            jax.ShapeDtypeStruct((own_count, rank), F32),
            jax.ShapeDtypeStruct((rank, columns), BF16),
        ),
        in_specs=[smem_spec(), vmem_spec(), vmem_spec()],
        out_specs=(any_spec(), any_spec()),
        scratch_shapes=[
            pltpu.VMEM((rank, rows), BF16),
            pltpu.VMEM((rank, columns), BF16),
            pltpu.VMEM((rank, columns), BF16),
            pltpu.VMEM((rank, rank), F32),
            pltpu.VMEM((rank, rank), F32),
            pltpu.VMEM((BLOCK, 2 * BLOCK), F32),
            pltpu.VMEM((own_count, rank), F32),
            pltpu.VMEM((rank, columns), BF16),
            pltpu.SemaphoreType.DMA((columns // TILE + 1,)),
        ],
        compiler_params=params(),
        name="final",
    )(start, weight_block, sketch)
    return (basis[None], factors[None])


def solution(mesh):
    placed = (P("ep", None, "tp"), P("ep", "tp", None), P())
    return jax.shard_map(
        per_device,
        mesh=mesh,
        in_specs=placed,
        out_specs=(P("ep", "tp", None), P("ep", None, "tp")),
        check_vma=False,
    )
```

```python
import math

import jax
import jax.numpy as jnp
from jax import lax
from jax.experimental import pallas as pl
from jax.experimental.pallas import tpu as pltpu
from jax.sharding import PartitionSpec as P

D = 7168
FF = 2048
POWER = 2
F32 = jnp.float32
BF16 = jnp.bfloat16
HIGHEST = lax.Precision.HIGHEST
BLOCK = 128
TILE = 256
VMEM_LIMIT = 24 * 1024 * 1024


def params():
    return pltpu.CompilerParams(vmem_limit_bytes=VMEM_LIMIT)


def vmem_spec():
    return pl.BlockSpec(memory_space=pltpu.VMEM)


def any_spec():
    return pl.BlockSpec(memory_space=pl.ANY)


def smem_spec():
    return pl.BlockSpec(memory_space=pltpu.SMEM)


def mm(a, b):
    return jnp.dot(a, b, preferred_element_type=F32)


def first_kernel(weights, probes, out):
    for s in range(0, out.shape[0], 2 * TILE):
        out[s : s + 2 * TILE, :] = mm(weights[s : s + 2 * TILE, :], probes[...]).astype(BF16)


def power_kernel(weights, sketch, out, turned, back):
    turned[...] = sketch[...].T
    for s in range(0, weights.shape[1], TILE):
        back[s : s + TILE, :] = mm(turned[...], weights[:, s : s + TILE]).astype(BF16).T
    for s in range(0, out.shape[0], 2 * TILE):
        rows = weights[s : s + 2 * TILE, :]
        out[s : s + 2 * TILE, :] = (mm(rows, back[...]) * (1.0 / D)).astype(BF16)


def pair_kernel(pairing, received, out):
    tp_count = out.shape[0] // pairing.shape[0]

    def total(expert):
        rows = received[pl.ds(expert * tp_count, tp_count)].astype(F32)
        return jnp.sum(rows, axis=0)

    for i in range(pairing.shape[0] // 2):
        a = pairing[2 * i]
        b = pairing[2 * i + 1]
        both = (total(a) + total(b)).astype(BF16)
        spread = jnp.broadcast_to(both[None], (tp_count,) + both.shape)
        out[pl.ds(a * tp_count, tp_count)] = spread
        out[pl.ds(b * tp_count, tp_count)] = spread


def exact(a, b):
    return jnp.dot(a, b, precision=HIGHEST, preferred_element_type=F32)


def exact_turned(a, b):
    turned = (((0,), (0,)), ((), ()))
    return lax.dot_general(a, b, turned, precision=HIGHEST, preferred_element_type=F32)


def identity(n):
    rows = lax.broadcasted_iota(jnp.int32, (n, n), 0)
    columns = lax.broadcasted_iota(jnp.int32, (n, n), 1)
    return jnp.where(rows == columns, 1.0, 0.0).astype(F32)


def factor_block(work, solved_rows, beside):
    lanes = work.shape[0]
    halves = range(work.shape[1] // lanes)
    count = lanes // 8
    sublane = lax.broadcasted_iota(jnp.int32, (8, lanes), 0)
    ones = jnp.ones((8, lanes), F32)

    def row(x, i):
        return jnp.broadcast_to(x[i : i + 1, :], x.shape)

    def column(x, c):
        return jnp.broadcast_to(x[:, c : c + 1], x.shape)

    def place(g, h):
        return slice(8 * g, 8 * g + 8), slice(lanes * h, lanes * h + lanes)

    panel = [[work[place(g, h)] for h in halves] for g in range(2)]
    for p in range(0, count, 2):
        if beside:
            beside.pop(0)()
        base = 8 * p
        reduced = [list(panel[0]), list(panel[1])]
        final = [list(panel[0]), list(panel[1])]
        columns = [[column(panel[q][0], base + i) for q in range(2)] for i in range(16)]
        inverses = [ones, ones]
        pivots = [ones, ones]
        for i in range(16):
            q, r = divmod(i, 8)
            pivot = row(columns[i][q], r)
            inverse = 1.0 / pivot
            pivots[q] = jnp.where(sublane == r, pivot, pivots[q])
            inverses[q] = jnp.where(sublane == r, inverse, inverses[q])
            scaled = [columns[i][0] * inverse, columns[i][1] * inverse]
            scaled[q] = jnp.where(sublane == r, 0.0, scaled[q])
            for c in range(i + 1, 16):
                across = row(columns[c][q], r)
                columns[c] = [columns[c][k] - scaled[k] * across for k in range(2)]
            for h in halves:
                pivot_row = row(reduced[q][h], r)
                final[q][h] = jnp.where(sublane == r, pivot_row, final[q][h])
                for k in range(2):
                    reduced[k][h] = reduced[k][h] - scaled[k] * pivot_row
        for q in range(2):
            for h in halves:
                reduced[q][h] = reduced[q][h] * inverses[q]
        solved = [[row(reduced[c // 8][h], c % 8) for h in halves] for c in range(16)]
        panel = []
        for g in range(p + 2, min(p + 4, count)):
            below = [work[place(g, h)] for h in halves]
            left = [column(below[0], base + c) for c in range(16)]
            for h in halves:
                terms = [left[c] * solved[c][h] for c in range(16)]
                while len(terms) > 1:
                    terms = [terms[k] + terms[k + 1] for k in range(0, len(terms), 2)]
                below[h] = below[h] - terms[0]
            panel.append(below)
        rest = 8 * (p + 4)
        if rest < lanes:
            for q in range(2):
                for h in halves:
                    solved_rows[place(q, h)] = reduced[q][h]
            update = exact(work[rest:, base : base + 16], solved_rows[...])
            work[rest:, :] = work[rest:, :] - update
        for q in range(2):
            scale = lax.rsqrt(pivots[q])
            for h in halves:
                work[place(p + q, h)] = final[q][h] * scale
    while beside:
        beside.pop(0)()


def inverse_factor(gram, inverse, work, solved_rows, beside):
    n = BLOCK
    upper_left, lower_left = slice(0, n), slice(n, 2 * n)
    work[:, :n] = gram[upper_left, :n]
    work[:, n:] = identity(n)
    share = (len(beside) + 1) // 2
    factor_block(work, solved_rows, beside[:share])
    top = work[:, n:]
    cross = exact(top, gram[upper_left, n:])
    work[:, :n] = gram[lower_left, n:] - exact_turned(cross, cross)
    work[:, n:] = identity(n)

    def fill():
        inverse[upper_left, :n] = top
        inverse[upper_left, n:] = jnp.zeros((n, n), F32)
        inverse[lower_left, :n] = exact_turned(cross, top)

    factor_block(work, solved_rows, [fill] + beside[share:])
    bottom = work[:, n:]
    inverse[lower_left, :n] = -exact(bottom, inverse[lower_left, :n])
    inverse[lower_left, n:] = bottom


def final_kernel(
    start,
    weights,
    sketch,
    basis,
    factors,
    turned,
    high_part,
    low_part,
    gram,
    inverse,
    work,
    solved_rows,
    own_basis,
    own_factors,
    sems,
):
    columns = weights.shape[1]
    turned[...] = sketch[...].T
    gram[...] = mm(turned[...], sketch[...])

    def project(s):
        def run():
            product = mm(turned[...], weights[:, s : s + TILE])
            high = product.astype(BF16)
            high_part[:, s : s + TILE] = high
            low_part[:, s : s + TILE] = (product - high.astype(F32)).astype(BF16)

        return run

    pieces = [project(s) for s in range(0, columns, TILE)]
    inverse_factor(gram, inverse, work, solved_rows, pieces)
    high = inverse[...].astype(BF16)
    low = (inverse[...] - high.astype(F32)).astype(BF16)
    copies = []
    for n, s in enumerate(range(0, columns, TILE)):
        part = high_part[:, s : s + TILE]
        rest = mm(low, part) + mm(high, low_part[:, s : s + TILE])
        own_factors[:, s : s + TILE] = (mm(high, part) + rest).astype(BF16)
        place = pl.ds(s, TILE)
        copies.append(
            pltpu.make_async_copy(own_factors.at[:, place], factors.at[:, place], sems.at[n])
        )
        copies[-1].start()
    own_count = own_basis.shape[0]
    own = sketch[pl.ds(pl.multiple_of(start[0] * own_count, own_count), own_count), :]
    own_basis[...] = (mm(own, high.T) + mm(own, low.T)) * math.sqrt(FF)
    copies.append(pltpu.make_async_copy(own_basis, basis, sems.at[len(copies)]))
    copies[-1].start()
    for copy in copies:
        copy.wait()


def exchange(value):
    return lax.all_to_all(value, ("ep", "tp"), split_axis=0, concat_axis=0, tiled=True)


def per_device(weights, probes, pairing):
    weight_block = weights[0]
    probe_block = probes[0]
    rows, columns = weight_block.shape
    rank = probe_block.shape[1]
    device_count = lax.axis_size("ep") * lax.axis_size("tp")
    own_count = rows // lax.axis_size("tp")
    sketch_shape = jax.ShapeDtypeStruct((rows, rank), BF16)
    chunks = (device_count, rows // device_count, rank)

    def relay(partial_value):
        received = exchange(partial_value.reshape(chunks))
        paired = pl.pallas_call(
            pair_kernel,
            out_shape=jax.ShapeDtypeStruct(chunks, BF16),
            in_specs=[smem_spec(), vmem_spec()],
            out_specs=vmem_spec(),
            compiler_params=params(),
            name="pair",
        )(pairing, received)
        return exchange(paired).reshape(rows, rank)

    partial_value = pl.pallas_call(
        first_kernel,
        out_shape=sketch_shape,
        in_specs=[vmem_spec(), vmem_spec()],
        out_specs=vmem_spec(),
        compiler_params=params(),
        name="first",
    )(weight_block, probe_block)
    start = lax.axis_index("tp").reshape(1).astype(jnp.int32)
    partial_value, start = lax.optimization_barrier((partial_value, start))
    sketch = relay(partial_value)
    for _ in range(POWER):
        partial_value = pl.pallas_call(
            power_kernel,
            out_shape=sketch_shape,
            in_specs=[vmem_spec(), vmem_spec()],
            out_specs=vmem_spec(),
            scratch_shapes=[
                pltpu.VMEM((rank, rows), BF16),
                pltpu.VMEM((columns, rank), BF16),
            ],
            compiler_params=params(),
            name="power",
        )(weight_block, sketch)
        sketch = relay(partial_value)
    basis, factors = pl.pallas_call(
        final_kernel,
        out_shape=(
            jax.ShapeDtypeStruct((own_count, rank), F32),
            jax.ShapeDtypeStruct((rank, columns), BF16),
        ),
        in_specs=[smem_spec(), vmem_spec(), vmem_spec()],
        out_specs=(any_spec(), any_spec()),
        scratch_shapes=[
            pltpu.VMEM((rank, rows), BF16),
            pltpu.VMEM((rank, columns), BF16),
            pltpu.VMEM((rank, columns), BF16),
            pltpu.VMEM((rank, rank), F32),
            pltpu.VMEM((rank, rank), F32),
            pltpu.VMEM((BLOCK, 2 * BLOCK), F32),
            pltpu.VMEM((16, 2 * BLOCK), F32),
            pltpu.VMEM((own_count, rank), F32),
            pltpu.VMEM((rank, columns), BF16),
            pltpu.SemaphoreType.DMA((columns // TILE + 1,)),
        ],
        compiler_params=params(),
        name="final",
    )(start, weight_block, sketch)
    return (basis[None], factors[None])


def solution(mesh):
    placed = (P("ep", None, "tp"), P("ep", "tp", None), P())
    return jax.shard_map(
        per_device,
        mesh=mesh,
        in_specs=placed,
        out_specs=(P("ep", "tp", None), P("ep", None, "tp")),
        check_vma=False,
    )
```

```python
import math

import jax
import jax.numpy as jnp
from jax import lax
from jax.experimental import pallas as pl
from jax.experimental.pallas import tpu as pltpu
from jax.sharding import PartitionSpec as P

D = 7168
FF = 2048
POWER = 2
F32 = jnp.float32
BF16 = jnp.bfloat16
HIGHEST = lax.Precision.HIGHEST
BLOCK = 128
TILE = 256
VMEM_LIMIT = 24 * 1024 * 1024


def params():
    return pltpu.CompilerParams(vmem_limit_bytes=VMEM_LIMIT)


def vmem_spec():
    return pl.BlockSpec(memory_space=pltpu.VMEM)


def any_spec():
    return pl.BlockSpec(memory_space=pl.ANY)


def smem_spec():
    return pl.BlockSpec(memory_space=pltpu.SMEM)


def mm(a, b):
    return jnp.dot(a, b, preferred_element_type=F32)


def first_kernel(weights, probes, out):
    for s in range(0, out.shape[0], 2 * TILE):
        out[s : s + 2 * TILE, :] = mm(weights[s : s + 2 * TILE, :], probes[...]).astype(BF16)


def turn_and_multiply(sketch, turned, other):
    total = None
    for s in range(0, sketch.shape[0], 2 * TILE):
        part = sketch[s : s + 2 * TILE, :].T
        turned[:, s : s + 2 * TILE] = part
        product = mm(part, other[s : s + 2 * TILE, :TILE])
        total = product if total is None else total + product
    return total


def power_kernel(weights, sketch, out, turned, back):
    back[:TILE, :] = turn_and_multiply(sketch, turned, weights).astype(BF16).T
    for s in range(TILE, weights.shape[1], TILE):
        back[s : s + TILE, :] = mm(turned[...], weights[:, s : s + TILE]).astype(BF16).T
    for s in range(0, out.shape[0], 2 * TILE):
        rows = weights[s : s + 2 * TILE, :]
        out[s : s + 2 * TILE, :] = (mm(rows, back[...]) * (1.0 / D)).astype(BF16)


def pair_kernel(pairing, received, out):
    tp_count = out.shape[0] // pairing.shape[0]

    def total(expert):
        rows = received[pl.ds(expert * tp_count, tp_count)].astype(F32)
        return jnp.sum(rows, axis=0)

    for i in range(pairing.shape[0] // 2):
        a = pairing[2 * i]
        b = pairing[2 * i + 1]
        both = (total(a) + total(b)).astype(BF16)
        spread = jnp.broadcast_to(both[None], (tp_count,) + both.shape)
        out[pl.ds(a * tp_count, tp_count)] = spread
        out[pl.ds(b * tp_count, tp_count)] = spread


def exact(a, b):
    return jnp.dot(a, b, precision=HIGHEST, preferred_element_type=F32)


def exact_turned(a, b):
    turned = (((0,), (0,)), ((), ()))
    return lax.dot_general(a, b, turned, precision=HIGHEST, preferred_element_type=F32)


def identity(n):
    rows = lax.broadcasted_iota(jnp.int32, (n, n), 0)
    columns = lax.broadcasted_iota(jnp.int32, (n, n), 1)
    return jnp.where(rows == columns, 1.0, 0.0).astype(F32)


def factor_block(work, solved_rows, beside):
    lanes = work.shape[0]
    halves = range(work.shape[1] // lanes)
    count = lanes // 8
    sublane = lax.broadcasted_iota(jnp.int32, (8, lanes), 0)
    ones = jnp.ones((8, lanes), F32)

    def row(x, i):
        return jnp.broadcast_to(x[i : i + 1, :], x.shape)

    def column(x, c):
        return jnp.broadcast_to(x[:, c : c + 1], x.shape)

    def place(g, h):
        return slice(8 * g, 8 * g + 8), slice(lanes * h, lanes * h + lanes)

    panel = [[work[place(g, h)] for h in halves] for g in range(2)]
    for p in range(0, count, 2):
        if beside:
            beside.pop(0)()
        base = 8 * p
        reduced = [list(panel[0]), list(panel[1])]
        final = [list(panel[0]), list(panel[1])]
        columns = [[column(panel[q][0], base + i) for q in range(2)] for i in range(16)]
        inverses = [ones, ones]
        pivots = [ones, ones]
        for i in range(16):
            q, r = divmod(i, 8)
            pivot = row(columns[i][q], r)
            inverse = 1.0 / pivot
            pivots[q] = jnp.where(sublane == r, pivot, pivots[q])
            inverses[q] = jnp.where(sublane == r, inverse, inverses[q])
            scaled = [columns[i][0] * inverse, columns[i][1] * inverse]
            scaled[q] = jnp.where(sublane == r, 0.0, scaled[q])
            for c in range(i + 1, 16):
                across = row(columns[c][q], r)
                columns[c] = [columns[c][k] - scaled[k] * across for k in range(2)]
            for h in halves:
                pivot_row = row(reduced[q][h], r)
                final[q][h] = jnp.where(sublane == r, pivot_row, final[q][h])
                for k in range(2):
                    reduced[k][h] = reduced[k][h] - scaled[k] * pivot_row
        for q in range(2):
            for h in halves:
                reduced[q][h] = reduced[q][h] * inverses[q]
        solved = [[row(reduced[c // 8][h], c % 8) for h in halves] for c in range(16)]
        panel = []
        for g in range(p + 2, min(p + 4, count)):
            below = [work[place(g, h)] for h in halves]
            left = [column(below[0], base + c) for c in range(16)]
            for h in halves:
                terms = [left[c] * solved[c][h] for c in range(16)]
                while len(terms) > 1:
                    terms = [terms[k] + terms[k + 1] for k in range(0, len(terms), 2)]
                below[h] = below[h] - terms[0]
            panel.append(below)
        rest = 8 * (p + 4)
        if rest < lanes:
            for q in range(2):
                for h in halves:
                    solved_rows[place(q, h)] = reduced[q][h]
            update = exact(work[rest:, base : base + 16], solved_rows[...])
            work[rest:, :] = work[rest:, :] - update
        for q in range(2):
            scale = lax.rsqrt(pivots[q])
            for h in halves:
                work[place(p + q, h)] = final[q][h] * scale
    while beside:
        beside.pop(0)()


def inverse_factor(gram, inverse, work, solved_rows, beside):
    n = BLOCK
    upper_left, lower_left = slice(0, n), slice(n, 2 * n)
    share = (len(beside) + 1) // 2
    work[:, : 2 * n] = gram[upper_left, :]
    work[:, 2 * n :] = identity(n)
    factor_block(work, solved_rows, beside[:share])
    inverse[upper_left, :n] = work[:, 2 * n :]
    inverse[upper_left, n:] = jnp.zeros((n, n), F32)
    update = exact_turned(work[:, n : 2 * n], work[:, n:])
    work[:, :n] = gram[lower_left, n:] - update[:, :n]
    work[:, n : 2 * n] = -update[:, n:]
    work[:, 2 * n :] = identity(n)
    factor_block(work, solved_rows, beside[share:])
    inverse[lower_left, :] = work[:, n:]


def final_kernel(
    start,
    weights,
    sketch,
    basis,
    factors,
    turned,
    high_part,
    low_part,
    gram,
    inverse,
    work,
    solved_rows,
    own_basis,
    own_factors,
    sems,
):
    columns = weights.shape[1]
    gram[...] = turn_and_multiply(sketch, turned, sketch)

    def project(s):
        def run():
            product = mm(turned[...], weights[:, s : s + TILE])
            high = product.astype(BF16)
            high_part[:, s : s + TILE] = high
            low_part[:, s : s + TILE] = (product - high.astype(F32)).astype(BF16)

        return run

    pieces = [project(s) for s in range(0, columns, TILE)]
    inverse_factor(gram, inverse, work, solved_rows, pieces)
    high = inverse[...].astype(BF16)
    low = (inverse[...] - high.astype(F32)).astype(BF16)
    copies = []
    for n, s in enumerate(range(0, columns, TILE)):
        part = high_part[:, s : s + TILE]
        rest = mm(low, part) + mm(high, low_part[:, s : s + TILE])
        own_factors[:, s : s + TILE] = (mm(high, part) + rest).astype(BF16)
        place = pl.ds(s, TILE)
        copies.append(
            pltpu.make_async_copy(own_factors.at[:, place], factors.at[:, place], sems.at[n])
        )
        copies[-1].start()
    own_count = own_basis.shape[0]
    own = sketch[pl.ds(pl.multiple_of(start[0] * own_count, own_count), own_count), :]
    own_basis[...] = (mm(own, high.T) + mm(own, low.T)) * math.sqrt(FF)
    copies.append(pltpu.make_async_copy(own_basis, basis, sems.at[len(copies)]))
    copies[-1].start()
    for copy in copies:
        copy.wait()


def exchange(value):
    return lax.all_to_all(value, ("ep", "tp"), split_axis=0, concat_axis=0, tiled=True)


def per_device(weights, probes, pairing):
    weight_block = weights[0]
    probe_block = probes[0]
    rows, columns = weight_block.shape
    rank = probe_block.shape[1]
    device_count = lax.axis_size("ep") * lax.axis_size("tp")
    own_count = rows // lax.axis_size("tp")
    sketch_shape = jax.ShapeDtypeStruct((rows, rank), BF16)
    chunks = (device_count, rows // device_count, rank)

    def relay(partial_value):
        received = exchange(partial_value.reshape(chunks))
        paired = pl.pallas_call(
            pair_kernel,
            out_shape=jax.ShapeDtypeStruct(chunks, BF16),
            in_specs=[smem_spec(), vmem_spec()],
            out_specs=vmem_spec(),
            compiler_params=params(),
            name="pair",
        )(pairing, received)
        return exchange(paired).reshape(rows, rank)

    partial_value = pl.pallas_call(
        first_kernel,
        out_shape=sketch_shape,
        in_specs=[vmem_spec(), vmem_spec()],
        out_specs=vmem_spec(),
        compiler_params=params(),
        name="first",
    )(weight_block, probe_block)
    start = lax.axis_index("tp").reshape(1).astype(jnp.int32)
    partial_value, start = lax.optimization_barrier((partial_value, start))
    sketch = relay(partial_value)
    for _ in range(POWER):
        partial_value = pl.pallas_call(
            power_kernel,
            out_shape=sketch_shape,
            in_specs=[vmem_spec(), vmem_spec()],
            out_specs=vmem_spec(),
            scratch_shapes=[
                pltpu.VMEM((rank, rows), BF16),
                pltpu.VMEM((columns, rank), BF16),
            ],
            compiler_params=params(),
            name="power",
        )(weight_block, sketch)
        sketch = relay(partial_value)
    basis, factors = pl.pallas_call(
        final_kernel,
        out_shape=(
            jax.ShapeDtypeStruct((own_count, rank), F32),
            jax.ShapeDtypeStruct((rank, columns), BF16),
        ),
        in_specs=[smem_spec(), vmem_spec(), vmem_spec()],
        out_specs=(any_spec(), any_spec()),
        scratch_shapes=[
            pltpu.VMEM((rank, rows), BF16),
            pltpu.VMEM((rank, columns), BF16),
            pltpu.VMEM((rank, columns), BF16),
            pltpu.VMEM((rank, rank), F32),
            pltpu.VMEM((rank, rank), F32),
            pltpu.VMEM((BLOCK, 3 * BLOCK), F32),
            pltpu.VMEM((16, 3 * BLOCK), F32),
            pltpu.VMEM((own_count, rank), F32),
            pltpu.VMEM((rank, columns), BF16),
            pltpu.SemaphoreType.DMA((columns // TILE + 1,)),
        ],
        compiler_params=params(),
        name="final",
    )(start, weight_block, sketch)
    return (basis[None], factors[None])


def solution(mesh):
    placed = (P("ep", None, "tp"), P("ep", "tp", None), P())
    return jax.shard_map(
        per_device,
        mesh=mesh,
        in_specs=placed,
        out_specs=(P("ep", "tp", None), P("ep", None, "tp")),
        check_vma=False,
    )
```

```python
import math

import jax
import jax.numpy as jnp
from jax import lax
from jax.experimental import pallas as pl
from jax.experimental.pallas import tpu as pltpu
from jax.sharding import PartitionSpec as P

D = 7168
FF = 2048
POWER = 2
F32 = jnp.float32
BF16 = jnp.bfloat16
HIGHEST = lax.Precision.HIGHEST
BLOCK = 128
TILE = 256
VMEM_LIMIT = 24 * 1024 * 1024


def params():
    return pltpu.CompilerParams(vmem_limit_bytes=VMEM_LIMIT)


def vmem_spec():
    return pl.BlockSpec(memory_space=pltpu.VMEM)


def any_spec():
    return pl.BlockSpec(memory_space=pl.ANY)


def smem_spec():
    return pl.BlockSpec(memory_space=pltpu.SMEM)


def mm(a, b):
    return jnp.dot(a, b, preferred_element_type=F32)


def first_kernel(weights, probes, out):
    for s in range(0, out.shape[0], 2 * TILE):
        out[s : s + 2 * TILE, :] = mm(weights[s : s + 2 * TILE, :], probes[...]).astype(BF16)


def power_kernel(weights, sketch, out, turned, back):
    turned[...] = sketch[...].T
    for s in range(0, weights.shape[1], TILE):
        back[s : s + TILE, :] = mm(turned[...], weights[:, s : s + TILE]).astype(BF16).T
    for s in range(0, out.shape[0], 2 * TILE):
        rows = weights[s : s + 2 * TILE, :]
        out[s : s + 2 * TILE, :] = (mm(rows, back[...]) * (1.0 / D)).astype(BF16)


def pair_kernel(pairing, received, out):
    tp_count = out.shape[0] // pairing.shape[0]

    def total(expert):
        rows = received[pl.ds(expert * tp_count, tp_count)].astype(F32)
        return jnp.sum(rows, axis=0)

    for i in range(pairing.shape[0] // 2):
        a = pairing[2 * i]
        b = pairing[2 * i + 1]
        both = (total(a) + total(b)).astype(BF16)
        spread = jnp.broadcast_to(both[None], (tp_count,) + both.shape)
        out[pl.ds(a * tp_count, tp_count)] = spread
        out[pl.ds(b * tp_count, tp_count)] = spread


def exact(a, b):
    return jnp.dot(a, b, precision=HIGHEST, preferred_element_type=F32)


def exact_turned(a, b):
    turned = (((0,), (0,)), ((), ()))
    return lax.dot_general(a, b, turned, precision=HIGHEST, preferred_element_type=F32)


def identity(n):
    rows = lax.broadcasted_iota(jnp.int32, (n, n), 0)
    columns = lax.broadcasted_iota(jnp.int32, (n, n), 1)
    return jnp.where(rows == columns, 1.0, 0.0).astype(F32)


def factor_block(work, solved_rows, beside):
    lanes = work.shape[0]
    halves = range(work.shape[1] // lanes)
    count = lanes // 8
    sublane = lax.broadcasted_iota(jnp.int32, (8, lanes), 0)
    ones = jnp.ones((8, lanes), F32)

    def row(x, i):
        return jnp.broadcast_to(x[i : i + 1, :], x.shape)

    def column(x, c):
        return jnp.broadcast_to(x[:, c : c + 1], x.shape)

    def place(g, h):
        return slice(8 * g, 8 * g + 8), slice(lanes * h, lanes * h + lanes)

    panel = [[work[place(g, h)] for h in halves] for g in range(2)]
    for p in range(0, count, 2):
        if beside:
            beside.pop(0)()
        base = 8 * p
        reduced = [list(panel[0]), list(panel[1])]
        final = [list(panel[0]), list(panel[1])]
        columns = [[column(panel[q][0], base + i) for q in range(2)] for i in range(16)]
        inverses = [ones, ones]
        pivots = [ones, ones]
        for i in range(16):
            q, r = divmod(i, 8)
            pivot = row(columns[i][q], r)
            inverse = 1.0 / pivot
            pivots[q] = jnp.where(sublane == r, pivot, pivots[q])
            inverses[q] = jnp.where(sublane == r, inverse, inverses[q])
            scaled = [columns[i][0] * inverse, columns[i][1] * inverse]
            scaled[q] = jnp.where(sublane == r, 0.0, scaled[q])
            for c in range(i + 1, 16):
                across = row(columns[c][q], r)
                columns[c] = [columns[c][k] - scaled[k] * across for k in range(2)]
            for h in halves:
                pivot_row = row(reduced[q][h], r)
                final[q][h] = jnp.where(sublane == r, pivot_row, final[q][h])
                for k in range(2):
                    reduced[k][h] = reduced[k][h] - scaled[k] * pivot_row
        for q in range(2):
            for h in halves:
                reduced[q][h] = reduced[q][h] * inverses[q]
        solved = [[row(reduced[c // 8][h], c % 8) for h in halves] for c in range(16)]
        panel = []
        for g in range(p + 2, min(p + 4, count)):
            below = [work[place(g, h)] for h in halves]
            left = [column(below[0], base + c) for c in range(16)]
            for h in halves:
                terms = [left[c] * solved[c][h] for c in range(16)]
                while len(terms) > 1:
                    terms = [terms[k] + terms[k + 1] for k in range(0, len(terms), 2)]
                below[h] = below[h] - terms[0]
            panel.append(below)
        rest = 8 * (p + 4)
        if rest < lanes:
            for q in range(2):
                for h in halves:
                    solved_rows[place(q, h)] = reduced[q][h]
            update = exact(work[rest:, base : base + 16], solved_rows[...])
            work[rest:, :] = work[rest:, :] - update
        for q in range(2):
            scale = lax.rsqrt(pivots[q])
            for h in halves:
                work[place(p + q, h)] = final[q][h] * scale
    while beside:
        beside.pop(0)()


def inverse_factor(gram, inverse, work, solved_rows, beside):
    n = BLOCK
    upper_left, lower_left = slice(0, n), slice(n, 2 * n)
    work[:, :n] = gram[upper_left, :n]
    work[:, n:] = identity(n)
    share = (len(beside) + 1) // 2
    factor_block(work, solved_rows, beside[:share])
    top = work[:, n:]
    cross = exact(top, gram[upper_left, n:])
    work[:, :n] = gram[lower_left, n:] - exact_turned(cross, cross)
    work[:, n:] = identity(n)

    def fill():
        inverse[upper_left, :n] = top
        inverse[upper_left, n:] = jnp.zeros((n, n), F32)
        inverse[lower_left, :n] = exact_turned(cross, top)

    factor_block(work, solved_rows, [fill] + beside[share:])
    bottom = work[:, n:]
    inverse[lower_left, :n] = -exact(bottom, inverse[lower_left, :n])
    inverse[lower_left, n:] = bottom


def final_kernel(
    start,
    weights,
    sketch,
    basis,
    factors,
    turned,
    high_part,
    low_part,
    gram,
    inverse,
    work,
    solved_rows,
    own_basis,
    own_factors,
    sems,
):
    columns = weights.shape[1]
    turned[...] = sketch[...].T
    gram[...] = mm(turned[...], sketch[...])

    def project(s):
        def run():
            product = mm(turned[...], weights[:, s : s + TILE])
            high = product.astype(BF16)
            high_part[:, s : s + TILE] = high
            low_part[:, s : s + TILE] = (product - high.astype(F32)).astype(BF16)

        return run

    pieces = [project(s) for s in range(0, columns, TILE)]
    inverse_factor(gram, inverse, work, solved_rows, pieces)
    high = inverse[...].astype(BF16)
    low = (inverse[...] - high.astype(F32)).astype(BF16)
    copies = []
    own_count = own_basis.shape[0]
    own = sketch[pl.ds(pl.multiple_of(start[0] * own_count, own_count), own_count), :]
    own_basis[...] = (mm(own, high.T) + mm(own, low.T)) * math.sqrt(FF)
    copies.append(pltpu.make_async_copy(own_basis, basis, sems.at[len(copies)]))
    copies[-1].start()
    for n, s in enumerate(range(0, columns, TILE)):
        part = high_part[:, s : s + TILE]
        rest = mm(low, part) + mm(high, low_part[:, s : s + TILE])
        own_factors[:, s : s + TILE] = (mm(high, part) + rest).astype(BF16)
        place = pl.ds(s, TILE)
        copies.append(
            pltpu.make_async_copy(own_factors.at[:, place], factors.at[:, place], sems.at[n + 1])
        )
        copies[-1].start()
    for copy in copies:
        copy.wait()


def exchange(value):
    return lax.all_to_all(value, ("ep", "tp"), split_axis=0, concat_axis=0, tiled=True)


def per_device(weights, probes, pairing):
    weight_block = weights[0]
    probe_block = probes[0]
    rows, columns = weight_block.shape
    rank = probe_block.shape[1]
    device_count = lax.axis_size("ep") * lax.axis_size("tp")
    own_count = rows // lax.axis_size("tp")
    sketch_shape = jax.ShapeDtypeStruct((rows, rank), BF16)
    chunks = (device_count, rows // device_count, rank)

    def relay(partial_value):
        received = exchange(partial_value.reshape(chunks))
        paired = pl.pallas_call(
            pair_kernel,
            out_shape=jax.ShapeDtypeStruct(chunks, BF16),
            in_specs=[smem_spec(), vmem_spec()],
            out_specs=vmem_spec(),
            compiler_params=params(),
            name="pair",
        )(pairing, received)
        return exchange(paired).reshape(rows, rank)

    partial_value = pl.pallas_call(
        first_kernel,
        out_shape=sketch_shape,
        in_specs=[vmem_spec(), vmem_spec()],
        out_specs=vmem_spec(),
        compiler_params=params(),
        name="first",
    )(weight_block, probe_block)
    start = lax.axis_index("tp").reshape(1).astype(jnp.int32)
    partial_value, start = lax.optimization_barrier((partial_value, start))
    sketch = relay(partial_value)
    for _ in range(POWER):
        partial_value = pl.pallas_call(
            power_kernel,
            out_shape=sketch_shape,
            in_specs=[vmem_spec(), vmem_spec()],
            out_specs=vmem_spec(),
            scratch_shapes=[
                pltpu.VMEM((rank, rows), BF16),
                pltpu.VMEM((columns, rank), BF16),
            ],
            compiler_params=params(),
            name="power",
        )(weight_block, sketch)
        sketch = relay(partial_value)
    basis, factors = pl.pallas_call(
        final_kernel,
        out_shape=(
            jax.ShapeDtypeStruct((own_count, rank), F32),
            jax.ShapeDtypeStruct((rank, columns), BF16),
        ),
        in_specs=[smem_spec(), vmem_spec(), vmem_spec()],
        out_specs=(any_spec(), any_spec()),
        scratch_shapes=[
            pltpu.VMEM((rank, rows), BF16),
            pltpu.VMEM((rank, columns), BF16),
            pltpu.VMEM((rank, columns), BF16),
            pltpu.VMEM((rank, rank), F32),
            pltpu.VMEM((rank, rank), F32),
            pltpu.VMEM((BLOCK, 2 * BLOCK), F32),
            pltpu.VMEM((16, 2 * BLOCK), F32),
            pltpu.VMEM((own_count, rank), F32),
            pltpu.VMEM((rank, columns), BF16),
            pltpu.SemaphoreType.DMA((columns // TILE + 1,)),
        ],
        compiler_params=params(),
        name="final",
    )(start, weight_block, sketch)
    return (basis[None], factors[None])


def solution(mesh):
    placed = (P("ep", None, "tp"), P("ep", "tp", None), P())
    return jax.shard_map(
        per_device,
        mesh=mesh,
        in_specs=placed,
        out_specs=(P("ep", "tp", None), P("ep", None, "tp")),
        check_vma=False,
    )
```
